32 devices in a mesh: gx: 8 (over z, x), gy: 4 (over y, core).
Axes of the slice: x: 2, y: 2, z: 4, core: 2. Of those that a mesh axis runs over, the one named last changes fastest.
Arguments:
- starting_thermal_values: float32 [64, 512, 128], P('gx', 'gy'), may hold values from -6 to 6
- horizontal_boundary_transmission: float32 [64, 512], P('gx', 'gy'), may hold values from 0.5 to 4
- lateral_boundary_transmission: float32 [64, 512], P('gx', 'gy'), may hold values from 0.5 to 4
- zaxis_interface_weight: float32 [64, 512], P('gx', 'gy'), may hold values from 0.5 to 4
Outputs:
- updated: float32 [64, 512, 128], P('gx', 'gy')
The draws below stay inside these ranges and needn't reach their ends.
All inputs are finite; a program needn't handle non-finite values.
Results may differ from the reference program's by a relative error of at most 0.0045.
Values sent between devices are 32-bit elements; how exact they have to be, the bound alone decides.
A program may use at most 64 MiB of HBM per device.

```python
import math
import jax
import jax.numpy as jnp
from jax import lax

NZ = 128
NX = 64
NY = 512


def draw_starting_thermal_values(key, part):
    keys = jax.random.split(key, 4)
    first_waves = jax.random.randint(keys[0], (4,), 1, 4).astype(jnp.float32)
    second_waves = jax.random.randint(keys[1], (4,), 1, 4).astype(jnp.float32)
    depth_weights = 0.7 * jax.random.normal(keys[2], (4, NZ), jnp.float32)
    first_grid = (jnp.arange(NX).astype(jnp.float32) + 0.5) / NX
    second_grid = (jnp.arange(NY).astype(jnp.float32) + 0.5) / NY
    first_cosine = jnp.cos(jnp.pi * first_waves[:, None] * first_grid[None])
    second_cosine = jnp.cos(jnp.pi * second_waves[:, None] * second_grid[None])
    smooth = jnp.einsum('mi,mj,mz->ijz', first_cosine, second_cosine, depth_weights)
    rough = 0.5 * jax.random.normal(keys[3], (NX, NY, NZ), jnp.float32)
    return jnp.clip(smooth + rough, -6.0, 6.0)


def block_levels(stream_key, shape, cuts, least, high):
    loudness = 1.0
    for position, blocks in cuts:
        heights = jax.random.uniform(jax.random.fold_in(jax.random.fold_in(stream_key, 6), position), (blocks,), jnp.float32, least / len(cuts), high / len(cuts))
        loudness = loudness * jnp.repeat(jnp.exp(heights), shape[position] // blocks).reshape((-1,) + (1,) * (len(shape) - 1 - position))
    return loudness


def setup_inputs(seed: int = 0) -> dict:
    key_of = jax.random.split(jax.random.key(seed), 5)
    starting_thermal_values = draw_starting_thermal_values(jax.random.fold_in(key_of[4], 71), 0)
    horizontal_boundary_transmission = jnp.clip(jnp.exp(math.log(4.0) - 2.0794415 * jax.random.uniform(key_of[1], (NX, NY), jnp.float32) ** block_levels(key_of[1], (NX, NY), ((0, 8), (1, 4)), -0.2, 0.2)), 0.5, 4.0)
    lateral_boundary_transmission = jnp.clip(jnp.exp(math.log(4.0) - 2.0794415 * jax.random.uniform(key_of[2], (NX, NY), jnp.float32) ** block_levels(key_of[2], (NX, NY), ((0, 8), (1, 4)), -0.2, 0.2)), 0.5, 4.0)
    zaxis_interface_weight = jnp.clip(jnp.exp(math.log(4.0) - 2.0794415 * jax.random.uniform(key_of[3], (NX, NY), jnp.float32) ** block_levels(key_of[3], (NX, NY), ((0, 8), (1, 4)), -0.2, 0.2)), 0.5, 4.0)
    return {"starting_thermal_values": starting_thermal_values, "horizontal_boundary_transmission": horizontal_boundary_transmission, "lateral_boundary_transmission": lateral_boundary_transmission, "zaxis_interface_weight": zaxis_interface_weight}


leading_speed = 40000.0
trailing_speed = 40000.0
third_rate = 0.25


def thomas(lower, middle, upper, vectors):
    lower = jnp.broadcast_to(lower, vectors.shape)
    middle = jnp.broadcast_to(middle, vectors.shape)
    upper = jnp.broadcast_to(upper, vectors.shape)

    def forward(carried, current):
        ratio_before, value_before = carried
        low_row, middle_row, upper_row, value_row = current
        pivot = middle_row - low_row * ratio_before
        ratio_next = upper_row / pivot
        value_next = (value_row - low_row * value_before) / pivot
        return (ratio_next, value_next), (ratio_next, value_next)

    empty_row = jnp.zeros(vectors.shape[1:], jnp.float32)
    _, (ratios, partial_values) = lax.scan(forward, (empty_row, empty_row), (lower, middle, upper, vectors))

    def backward(after_row, current):
        ratio_row, value_row = current
        result = value_row - ratio_row * after_row
        return result, result

    _, solution = lax.scan(backward, empty_row, (ratios, partial_values), reverse=True)
    return solution


def face_rows(faces, rate):
    below = jnp.concatenate([jnp.zeros((1, faces.shape[1]), jnp.float32), faces[:-1]], 0)
    return -rate * below, 1.0 + rate * (below + faces), -rate * faces


def reference(starting_thermal_values, horizontal_boundary_transmission, lateral_boundary_transmission, zaxis_interface_weight):
    bordered_thermal_mesh = jnp.pad(starting_thermal_values, ((1, 1), (1, 1), (0, 0)))
    horizontal_below_band = jnp.concatenate([jnp.zeros((1, NY), jnp.float32), horizontal_boundary_transmission[:-1]], 0)
    lateral_below_band = jnp.concatenate([jnp.zeros((NX, 1), jnp.float32), lateral_boundary_transmission[:, :-1]], 1)
    inner_points = starting_thermal_values
    leading_flux = leading_speed * (horizontal_boundary_transmission[:, :, None] * (bordered_thermal_mesh[2:, 1:-1] - inner_points) - horizontal_below_band[:, :, None] * (inner_points - bordered_thermal_mesh[:-2, 1:-1]))
    trailing_flux = trailing_speed * (lateral_boundary_transmission[:, :, None] * (bordered_thermal_mesh[1:-1, 2:] - inner_points) - lateral_below_band[:, :, None] * (inner_points - bordered_thermal_mesh[1:-1, :-2]))
    increasing_ramp = starting_thermal_values[:, :, 1:] - starting_thermal_values[:, :, :-1]
    blank_vector_line = jnp.zeros((NX, NY, 1), jnp.float32)
    third_flow = third_rate * zaxis_interface_weight[:, :, None] * (jnp.concatenate([increasing_ramp, blank_vector_line], 2) - jnp.concatenate([blank_vector_line, increasing_ramp], 2))
    source = 2.0 * (leading_flux + trailing_flux + third_flow)

    first_lower, first_middle, first_upper = face_rows(horizontal_boundary_transmission, leading_speed)
    second_lower, second_middle, second_upper = face_rows(lateral_boundary_transmission.T, trailing_speed)

    def layered_slices(block):
        across = thomas(first_lower[:, :, None], first_middle[:, :, None], first_upper[:, :, None], block)
        turned = jnp.transpose(across, (1, 0, 2))
        along = thomas(second_lower[:, :, None], second_middle[:, :, None], second_upper[:, :, None], turned)
        return jnp.transpose(along, (1, 0, 2))

    blocks = jnp.transpose(source.reshape(NX, NY, NZ // 8, 8), (2, 0, 1, 3))
    after_second = jnp.transpose(lax.map(layered_slices, blocks), (1, 2, 0, 3)).reshape(NX, NY, NZ)

    depth = jnp.arange(NZ)
    low_mask = (depth >= 1).astype(jnp.float32)
    high_mask = (depth < NZ - 1).astype(jnp.float32)

    def columns(inputs_pair):
        slab_plane, vertical = inputs_pair
        rate_row = third_rate * vertical
        lower = -(low_mask[:, None] * rate_row[None])
        upper = -(high_mask[:, None] * rate_row[None])
        middle = 1.0 + (low_mask + high_mask)[:, None] * rate_row[None]
        return thomas(lower, middle, upper, slab_plane.T).T

    final_pass_result = lax.map(columns, (after_second, zaxis_interface_weight))
    return starting_thermal_values + final_pass_result
```

```python
import functools

import jax
import jax.numpy as jnp
import numpy as np
from jax import lax
from jax.experimental import pallas as pl
from jax.experimental.pallas import tpu as pltpu
from jax.sharding import PartitionSpec as P

R1 = 40000.0
R2 = 40000.0
R3 = 0.25
MESH = pl.DeviceIdType.MESH


def dot(a, b):
    return jnp.dot(a, b, precision=lax.Precision.HIGHEST, preferred_element_type=jnp.float32)


def kernel(
    dx, dy,
    u, p, q, w, basis, basis_t, mu, out,
    uh, xl, pall, gbuf, grecv, summ, rin, rout, zx, ysum, yall, ca, cat, cb, cbt, rho_s, ipi_s,
    scan_s, edge_s,
    p_send, p_recv, g_send, g_recv, a_send, a_recv, b_send, b_recv, y_send, y_recv,
):
    nx, ny, nz = u.shape
    chunk = ny // dx
    mx, my = lax.axis_index("gx"), lax.axis_index("gy")

    gbuf[0] = u[:, 0, :]
    gbuf[1] = u[:, ny - 1, :]
    gbuf[2] = q[...]

    barrier = pltpu.get_barrier_semaphore()
    for off in range(1, dx):
        pl.semaphore_signal(
            barrier, inc=1, device_id={"gx": lax.rem(mx + off, dx)}, device_id_type=MESH
        )
    for off in range(1, dy):
        pl.semaphore_signal(
            barrier, inc=1, device_id={"gy": lax.rem(my + off, dy)}, device_id_type=MESH
        )
    pl.semaphore_wait(barrier, dx + dy - 2)

    def send(src, dst, ssem, rsem, axis, peer):
        copy = pltpu.make_async_remote_copy(
            src_ref=src, dst_ref=dst, send_sem=ssem, recv_sem=rsem,
            device_id={axis: peer}, device_id_type=MESH,
        )
        copy.start()
        return copy

    p_copies = [
        send(p, pall.at[mx], p_send.at[o], p_recv.at[o], "gx", lax.rem(mx + o, dx))
        for o in range(1, dx)
    ]
    g_copies = [
        send(gbuf, grecv.at[my], g_send.at[o], g_recv.at[o], "gy", lax.rem(my + o, dy))
        for o in range(1, dy)
    ]
    pall[mx] = p[...]
    grecv[my] = gbuf[...]

    uh[...] = dot(u[...].reshape(nx * ny, nz), basis[...]).reshape(nx, ny, nz)

    for copy in g_copies:
        copy.wait()

    g = R2 * grecv[:, 2].reshape(dy * nx, ny)
    lane = lax.broadcasted_iota(jnp.int32, (dy * nx, ny), 1)
    scale = 1.0 / (2.0 + 3.0 * g)
    a, b, c, d = (1.0 + g) * scale, g * scale, scale, g * scale
    stride = 1
    while stride < ny:
        ar, br, cr, dr = (pltpu.roll(m, stride, 1) for m in (a, b, c, d))
        na, nb, nc, nd = a * ar + b * cr, a * br + b * dr, c * ar + d * cr, c * br + d * dr
        scale = 1.0 / (na + nb + nc + nd)
        keep = lane >= stride
        a, b, c, d = (
            jnp.where(keep, n * scale, o)
            for n, o in ((na, a), (nb, b), (nc, c), (nd, d))
        )
        stride *= 2
    sigma_in = jnp.ones((nx, 1), jnp.float32)
    for k in range(dy - 1):
        rows = slice(k * nx, (k + 1) * nx)
        ta, tb, tc, td = (m[rows, ny - 1 :] for m in (a, b, c, d))
        sigma_in = jnp.where(
            k < my, (ta * sigma_in + tb) / (tc * sigma_in + td), sigma_in
        )
    for k, m in enumerate((a, b, c, d)):
        scan_s[k] = pltpu.roll(m, 1, 1).reshape(dy, nx, ny)
    lane = lax.broadcasted_iota(jnp.int32, (nx, ny), 1)
    a, b, c, d = (scan_s[k, my] for k in range(4))
    sigma = jnp.where(lane == 0, sigma_in, (a * sigma_in + b) / (c * sigma_in + d))
    g = R2 * q[...]
    ipi = 1.0 / (g + sigma)
    prefix = g * ipi
    stride = 1
    while stride < ny:
        prefix = jnp.where(lane >= stride, prefix * pltpu.roll(prefix, stride, 1), prefix)
        stride *= 2
    total = prefix[:, ny - 1 :]
    before = jnp.where(lane == 0, 1.0, pltpu.roll(prefix, 1, 1))
    inverse = 1.0 / before
    row_i = lax.broadcasted_iota(jnp.int32, (ny, ny), 0)
    col_i = lax.broadcasted_iota(jnp.int32, (ny, ny), 1)
    lower = jnp.where(row_i >= col_i, 1.0, 0.0)
    upper = jnp.where(row_i <= col_i, 1.0, 0.0)
    weight = before * before * ipi
    a2 = inverse * dot(weight, lower)
    b2 = inverse * total
    cb[...] = jnp.zeros_like(cb)
    for k, m in enumerate((g, R3 * w[...], inverse, weight, a2, b2)):
        cb[k * nx : (k + 1) * nx] = m
    cbt[...] = cb[...].T

    ysum[2] = jnp.broadcast_to(total, (nx, nz))
    ysum[3] = jnp.broadcast_to(a2[:, 0:1], (nx, nz))

    prev, following = lax.rem(my + dy - 1, dy), lax.rem(my + 1, dy)
    low_u = dot(grecv[prev, 1], basis[...])
    high_u = jnp.where(my == dy - 1, 0.0, dot(grecv[following, 0], basis[...]))
    q_before = jnp.where(my == 0, 0.0, R2 * grecv[prev, 2][:, ny - 1 :])
    first_u = dot(gbuf[0], basis[...])
    edge_s[0] = q_before * (first_u - low_u)
    edge_s[1] = high_u

    for copy in p_copies:
        copy.wait()
    sigma = jnp.ones((1, ny), jnp.float32)
    for k in range(dx):
        block = R1 * pall[k]
        rhos, ipis = [], []
        for r in range(nx):
            gr = block[r : r + 1]
            inv = 1.0 / (gr + sigma)
            rho = gr * inv
            sigma = 1.0 + rho * sigma
            rhos.append(rho)
            ipis.append(inv)
        rho_s[k] = jnp.concatenate(rhos, 0)
        ipi_s[k] = jnp.concatenate(ipis, 0)

    def responses(rho, ipi):
        prod = [jnp.ones_like(rho[0])]
        for r in range(nx):
            prod.append(prod[r] * rho[r])
        resp, tail = [None] * nx, [None] * nx
        resp[nx - 1], tail[nx - 1] = prod[nx - 1] * ipi[nx - 1], rho[nx - 1]
        for r in range(nx - 2, -1, -1):
            resp[r] = prod[r] * ipi[r] + rho[r] * resp[r + 1]
            tail[r] = rho[r] * tail[r + 1]
        return resp, tail

    resp, tail = responses(
        [rho_s[:, r, :] for r in range(nx)], [ipi_s[:, r, :] for r in range(nx)]
    )
    ca[...] = jnp.zeros_like(ca)
    base = 4 * nx
    ca[base : base + dx] = tail[0]
    ca[base + dx : base + 2 * dx] = resp[0]
    rho, ipi = rho_s[mx], ipi_s[mx]
    resp, tail = responses(
        [rho[r : r + 1] for r in range(nx)], [ipi[r : r + 1] for r in range(nx)]
    )
    ca[0:nx] = rho
    ca[nx : 2 * nx] = ipi
    ca[2 * nx : 3 * nx] = jnp.concatenate(resp, 0)
    ca[3 * nx : 4 * nx] = jnp.concatenate(tail, 0)
    cat[...] = ca[...].T

    row = lax.broadcasted_iota(jnp.int32, (ny, nz), 0)
    z = None
    for r in range(nx):
        v = uh[r]
        gc = cbt[:, r : r + 1]
        wc = cbt[:, nx + r : nx + r + 1]
        after = jnp.where(row == ny - 1, edge_s[1, r : r + 1, :], pltpu.roll(v, ny - 1, 0))
        flux = gc * (after - v)
        flux_before = jnp.where(row == 0, edge_s[0, r : r + 1, :], pltpu.roll(flux, 1, 0))
        h = (flux - flux_before) + (v - (wc * mu[...]) * v)
        z = h if r == 0 else h + cat[:, r - 1 : r] * z
        xl[r] = z
    summ[0] = cat[:, nx - 1 : nx] * z
    x = z * cat[:, 2 * nx - 1 : 2 * nx]
    xl[nx - 1] = x
    for r in range(nx - 2, -1, -1):
        x = xl[r] * cat[:, nx + r : nx + r + 1] + cat[:, r : r + 1] * x
        xl[r] = x
    summ[1] = x

    def part(index):
        return pl.ds(pl.multiple_of(index * chunk, chunk), chunk)

    copies = []
    for o in range(1, dx):
        peer = lax.rem(mx + o, dx)
        copies.append(
            send(summ.at[:, part(peer), :], rin.at[mx], a_send.at[o], a_recv.at[o], "gx", peer)
        )
    rin[mx] = summ[:, part(mx), :]
    for copy in copies:
        copy.wait()
    own = cat[part(mx), :]
    carry = jnp.zeros((chunk, nz), jnp.float32)
    carries = []
    for k in range(dx):
        carries.append(carry)
        rout[k, 0] = carry
        carry = rin[k, 0] + own[:, base + k : base + k + 1] * carry
    carry = jnp.zeros((chunk, nz), jnp.float32)
    for k in range(dx - 1, -1, -1):
        rout[k, 1] = carry
        carry = (
            rin[k, 1]
            + own[:, base + dx + k : base + dx + k + 1] * carries[k]
            + own[:, base + k : base + k + 1] * carry
        )
    copies = []
    for o in range(1, dx):
        peer = lax.rem(mx + o, dx)
        copies.append(
            send(rout.at[peer], zx.at[:, part(mx), :], b_send.at[o], b_recv.at[o], "gx", peer)
        )
    zx[:, part(mx), :] = rout[mx]
    for copy in copies:
        copy.wait()

    for r in range(nx):
        x = (
            xl[r]
            + cat[:, 2 * nx + r : 2 * nx + r + 1] * zx[0]
            + cat[:, 3 * nx + r : 3 * nx + r + 1] * zx[1]
        )
        f = 2.0 * (x - uh[r])
        inv = cbt[:, 2 * nx + r : 2 * nx + r + 1]
        s = dot(lower, inv * f)
        ysum[0, r : r + 1, :] = s[ny - 1 :]
        y = inv * dot(upper, cbt[:, 3 * nx + r : 3 * nx + r + 1] * s)
        ysum[1, r : r + 1, :] = y[0:1]
        xl[r] = y
    copies = [
        send(ysum, yall.at[my], y_send.at[o], y_recv.at[o], "gy", lax.rem(my + o, dy))
        for o in range(1, dy)
    ]
    yall[my] = ysum[...]
    for copy in copies:
        copy.wait()
    carry = jnp.zeros((nx, nz), jnp.float32)
    zeta, carries = carry, []
    for k in range(dy):
        carries.append(carry)
        zeta = jnp.where(k == my, carry, zeta)
        carry = yall[k, 2] * (yall[k, 0] + carry)
    carry = jnp.zeros((nx, nz), jnp.float32)
    xi = carry
    for k in range(dy - 1, -1, -1):
        xi = jnp.where(k == my, carry, xi)
        carry = yall[k, 1] + yall[k, 3] * carries[k] + yall[k, 2] * carry

    for r in range(nx):
        v = (
            xl[r]
            + cbt[:, 4 * nx + r : 4 * nx + r + 1] * zeta[r : r + 1]
            + cbt[:, 5 * nx + r : 5 * nx + r + 1] * xi[r : r + 1]
        )
        v = v / (1.0 + cbt[:, nx + r : nx + r + 1] * mu[...])
        out[r] = u[r] + dot(v, basis_t[...])


def shards(dx, dy, u, p, q, w):
    nx, ny, nz = u.shape
    mode = np.arange(nz)
    basis = np.cos(np.pi * mode[None, :] * (mode[:, None] + 0.5) / nz) * np.sqrt(2.0 / nz)
    basis[:, 0] *= np.sqrt(0.5)
    mu = (2.0 - 2.0 * np.cos(np.pi * mode / nz))[None, :]
    basis_t = jnp.asarray(basis.T, jnp.float32)
    basis = jnp.asarray(basis, jnp.float32)
    mu = jnp.asarray(mu, jnp.float32)
    chunk = ny // dx
    f32 = lambda *shape: pltpu.VMEM(shape, jnp.float32)
    rows = -(-(4 * nx + 2 * dx) // 128) * 128
    sems = []
    for count in (dx, dy, dx, dx, dy):
        sems += [pltpu.SemaphoreType.DMA((count,))] * 2
    vmem = pl.BlockSpec(memory_space=pltpu.VMEM)
    return pl.pallas_call(
        functools.partial(kernel, dx, dy),
        out_shape=jax.ShapeDtypeStruct(u.shape, jnp.float32),
        in_specs=[vmem] * 7,
        out_specs=vmem,
        scratch_shapes=[
            f32(nx, ny, nz), f32(nx, ny, nz), f32(dx, nx, ny), f32(3, nx, ny),
            f32(dy, 3, nx, ny), f32(2, ny, nz), f32(dx, 2, chunk, nz), f32(dx, 2, chunk, nz),
            f32(2, ny, nz), f32(4, nx, nz), f32(dy, 4, nx, nz),
            f32(rows, ny), f32(ny, rows), f32(rows, ny), f32(ny, rows),
            f32(dx, nx, ny), f32(dx, nx, ny), f32(4, dy, nx, ny), f32(2, nx, nz),
        ] + sems,
        compiler_params=pltpu.CompilerParams(
            collective_id=0, has_side_effects=True, vmem_limit_bytes=48 * 2**20
        ),
    )(u, p, q, w, basis, basis_t, mu)


def solution(mesh):
    dx, dy = mesh.shape["gx"], mesh.shape["gy"]
    in_specs = (P("gx", "gy", None), P("gx", "gy"), P("gx", "gy"), P("gx", "gy"))
    return jax.shard_map(
        functools.partial(shards, dx, dy), mesh=mesh, in_specs=in_specs,
        out_specs=P("gx", "gy", None), check_vma=False,
    )
```

```python
import functools

import jax
import jax.numpy as jnp
import numpy as np
from jax import lax
from jax.experimental import pallas as pl
from jax.experimental.pallas import tpu as pltpu
from jax.sharding import PartitionSpec as P

R1 = 40000.0
R2 = 40000.0
R3 = 0.25
MESH = pl.DeviceIdType.MESH


def dot(a, b):
    return jnp.dot(a, b, precision=lax.Precision.HIGHEST, preferred_element_type=jnp.float32)


def kernel(
    dx, dy,
    u_h, p_h, q_h, w_h, consts_h, out,
    u, p, q, w, consts,
    uh, xl, gbuf, grecv, ybuf, yrecv, nbuf, nrecv, summ, rin, rout, zx, ysum, yall,
    ca, cat, cb, cbt, co, cot,
    in_sem, n_send, n_recv, g_send, g_recv, c_send, c_recv,
    a_send, a_recv, b_send, b_recv, y_send, y_recv,
):
    nx, ny, nz = u.shape
    chunk = ny // dx
    mx, my = lax.axis_index("gx"), lax.axis_index("gy")
    far_first = sorted(range(1, dx), key=lambda o: abs(2 * o - dx))

    barrier = pltpu.get_barrier_semaphore()
    for off in far_first:
        pl.semaphore_signal(
            barrier, inc=1, device_id={"gx": lax.rem(mx + off, dx)}, device_id_type=MESH
        )
    for off in range(1, dy):
        pl.semaphore_signal(
            barrier, inc=1, device_id={"gy": lax.rem(my + off, dy)}, device_id_type=MESH
        )
    loads = []
    for k, (src, dst) in enumerate(
        ((q_h, q), (p_h, p), (w_h, w), (consts_h, consts), (u_h, u))
    ):
        loads.append(pltpu.make_async_copy(src, dst, in_sem.at[k]))
        loads[k].start()

    def send(src, dst, ssem, rsem, axis, peer):
        copy = pltpu.make_async_remote_copy(
            src_ref=src, dst_ref=dst, send_sem=ssem, recv_sem=rsem,
            device_id={axis: peer}, device_id_type=MESH,
        )
        copy.start()
        return copy

    for k in range(3):
        loads[k].wait()

    g = R2 * q[...]
    lane = lax.broadcasted_iota(jnp.int32, (nx, ny), 1)
    scale = 1.0 / (2.0 + 3.0 * g)
    a, b, c, d = (1.0 + g) * scale, g * scale, scale, g * scale
    stride = 1
    while stride < ny:
        ar, br, cr, dr = (pltpu.roll(m, stride, 1) for m in (a, b, c, d))
        na, nb, nc, nd = a * ar + b * cr, a * br + b * dr, c * ar + d * cr, c * br + d * dr
        scale = 1.0 / (na + nb + nc + nd)
        keep = lane >= stride
        a, b, c, d = (
            jnp.where(keep, n * scale, o)
            for n, o in ((na, a), (nb, b), (nc, c), (nd, d))
        )
        stride *= 2
    sigma = jnp.where(lane == 0, 1.0, pltpu.roll((a + b) / (c + d), 1, 1))
    ipi = 1.0 / (g + sigma)
    rho = g * ipi
    prefix = rho
    stride = 1
    while stride < ny:
        prefix = jnp.where(lane >= stride, prefix * pltpu.roll(prefix, stride, 1), prefix)
        stride *= 2
    total = prefix[:, ny - 1 :]
    before = jnp.where(lane == 0, 1.0, pltpu.roll(prefix, 1, 1))
    inverse = 1.0 / before
    row_i = lax.broadcasted_iota(jnp.int32, (ny, ny), 0)
    col_i = lax.broadcasted_iota(jnp.int32, (ny, ny), 1)
    lower = jnp.where(row_i >= col_i, 1.0, 0.0)
    upper = jnp.where(row_i <= col_i, 1.0, 0.0)
    weight = before * before * ipi
    a2 = inverse * dot(weight, lower)
    b2 = inverse * total
    cb[...] = jnp.zeros_like(cb)
    for k, m in enumerate((g, R3 * w[...], inverse, weight, a2, b2)):
        cb[k * nx : (k + 1) * nx] = m
    cbt[...] = cb[...].T
    ybuf[0] = jnp.broadcast_to(total, (nx, nz))
    ybuf[1] = jnp.broadcast_to(a2[:, 0:1], (nx, nz))
    ybuf[2] = jnp.broadcast_to((rho * sigma)[:, ny - 1 :], (nx, nz))

    gp = R1 * p[...]
    sigma = jnp.ones((1, ny), jnp.float32)
    rhos, ipis, prod = [], [], [sigma]
    for r in range(nx):
        gr = gp[r : r + 1]
        inv = 1.0 / (gr + sigma)
        rhos.append(gr * inv)
        ipis.append(inv)
        leak = rhos[r] * sigma
        sigma = 1.0 + leak
        prod.append(prod[r] * rhos[r])
    resp, tail = [None] * nx, [None] * nx
    resp[nx - 1], tail[nx - 1] = prod[nx - 1] * ipis[nx - 1], rhos[nx - 1]
    for r in range(nx - 2, -1, -1):
        resp[r] = prod[r] * ipis[r] + rhos[r] * resp[r + 1]
        tail[r] = rhos[r] * tail[r + 1]
    ca[...] = jnp.zeros_like(ca)
    for k, m in enumerate((rhos, ipis, resp, tail)):
        ca[k * nx : (k + 1) * nx] = jnp.concatenate(m, 0)
    cat[...] = ca[...].T
    nbuf[...] = jnp.zeros_like(nbuf)
    nbuf[0:1] = tail[0]
    nbuf[1:2] = resp[0]
    nbuf[2:3] = leak

    loads[3].wait()
    loads[4].wait()
    basis = consts[0:nz]
    mu = consts[nz : nz + 1]
    gbuf[0] = u[:, 0, :]
    gbuf[1] = u[:, ny - 1, :]
    gbuf[2] = q[...]
    uh[...] = dot(u[...].reshape(nx * ny, nz), basis).reshape(nx, ny, nz)

    pl.semaphore_wait(barrier, dx + dy - 2)
    g_copies = [
        send(gbuf, grecv.at[my], g_send.at[o], g_recv.at[o], "gy", lax.rem(my + o, dy))
        for o in sorted({1, dy - 1})
    ]
    n_copies = [
        send(nbuf, nrecv.at[mx], n_send.at[o], n_recv.at[o], "gx", lax.rem(mx + o, dx))
        for o in far_first
    ]
    c_copies = [
        send(ybuf, yrecv.at[my], c_send.at[o], c_recv.at[o], "gy", lax.rem(my + o, dy))
        for o in range(1, dy)
    ]
    nrecv[mx] = nbuf[...]
    yrecv[my] = ybuf[...]
    first_u = dot(gbuf[0], basis)
    for copy in g_copies:
        copy.wait()

    prev, following = lax.rem(my + dy - 1, dy), lax.rem(my + 1, dy)
    low_u = dot(grecv[prev, 1], basis)
    high_u = jnp.where(my == dy - 1, 0.0, dot(grecv[following, 0], basis))
    q_before = jnp.where(my == 0, 0.0, R2 * grecv[prev, 2][:, ny - 1 :])
    low_flux = q_before * (first_u - low_u)

    row = lax.broadcasted_iota(jnp.int32, (ny, nz), 0)
    z = None
    for r in range(nx):
        v = uh[r]
        gc = cbt[:, r : r + 1]
        wc = cbt[:, nx + r : nx + r + 1]
        after = jnp.where(row == ny - 1, high_u[r : r + 1], pltpu.roll(v, ny - 1, 0))
        flux = gc * (after - v)
        flux_before = jnp.where(row == 0, low_flux[r : r + 1], pltpu.roll(flux, 1, 0))
        h = (flux - flux_before) + (v - (wc * mu) * v)
        z = h if r == 0 else h + cat[:, r - 1 : r] * z
        xl[r] = z
    summ[0] = cat[:, nx - 1 : nx] * z
    x = z * cat[:, 2 * nx - 1 : 2 * nx]
    xl[nx - 1] = x
    for r in range(nx - 2, -1, -1):
        x = xl[r] * cat[:, nx + r : nx + r + 1] + cat[:, r : r + 1] * x
        xl[r] = x
    summ[1] = x

    def part(index):
        return pl.ds(pl.multiple_of(index * chunk, chunk), chunk)

    copies = []
    for o in far_first:
        peer = lax.rem(mx + o, dx)
        copies.append(
            send(summ.at[:, part(peer), :], rin.at[mx], a_send.at[o], a_recv.at[o], "gx", peer)
        )
    rin[mx] = summ[:, part(mx), :]

    for copy in n_copies:
        copy.wait()
    co[...] = jnp.zeros_like(co)
    tau = jnp.zeros((1, ny), jnp.float32)
    for k in range(dx):
        link, answer, leak = nrecv[k, 0:1], nrecv[k, 1:2], nrecv[k, 2:3]
        inv = 1.0 / (1.0 + answer * tau)
        co[5 * k : 5 * k + 1] = link * inv
        co[5 * k + 1 : 5 * k + 2] = link * inv * tau
        co[5 * k + 2 : 5 * k + 3] = inv
        co[5 * k + 3 : 5 * k + 4] = inv * answer
        co[5 * k + 4 : 5 * k + 5] = tau
        tau = leak + link * link * inv * tau
    cot[...] = co[...].T
    own = cot[part(mx), :]
    col = lambda k, m: own[:, 5 * k + m : 5 * k + m + 1]
    for copy in copies:
        copy.wait()
    carry = jnp.zeros((chunk, nz), jnp.float32)
    carries = []
    for k in range(dx):
        carries.append(carry)
        carry = rin[k, 0] + col(k, 0) * carry - col(k, 1) * rin[k, 1]
    carry = jnp.zeros((chunk, nz), jnp.float32)
    for k in range(dx - 1, -1, -1):
        rout[k, 1] = carry
        carry = col(k, 2) * rin[k, 1] + col(k, 3) * carries[k] + col(k, 0) * carry
        rout[k, 0] = carries[k] - col(k, 4) * carry
    copies = []
    for o in far_first:
        peer = lax.rem(mx + o, dx)
        copies.append(
            send(rout.at[peer], zx.at[:, part(mx), :], b_send.at[o], b_recv.at[o], "gx", peer)
        )
    zx[:, part(mx), :] = rout[mx]
    for copy in copies:
        copy.wait()

    for r in range(nx):
        x = (
            xl[r]
            + cat[:, 2 * nx + r : 2 * nx + r + 1] * zx[0]
            + cat[:, 3 * nx + r : 3 * nx + r + 1] * zx[1]
        )
        f = 2.0 * (x - uh[r])
        inv = cbt[:, 2 * nx + r : 2 * nx + r + 1]
        s = dot(lower, inv * f)
        ysum[0, r : r + 1, :] = s[ny - 1 :]
        y = inv * dot(upper, cbt[:, 3 * nx + r : 3 * nx + r + 1] * s)
        ysum[1, r : r + 1, :] = y[0:1]
        xl[r] = y
    copies = [
        send(ysum, yall.at[my], y_send.at[o], y_recv.at[o], "gy", lax.rem(my + o, dy))
        for o in range(1, dy)
    ]
    yall[my] = ysum[...]
    for copy in copies + c_copies:
        copy.wait()
    carry = jnp.zeros((nx, nz), jnp.float32)
    tau, carries, taus, invs = carry, [], [], []
    for k in range(dy):
        link = yrecv[k, 0]
        inv = 1.0 / (1.0 + yrecv[k, 1] * tau)
        carries.append(carry)
        taus.append(tau)
        invs.append(inv)
        carry = link * (yall[k, 0] + inv * (carry - tau * yall[k, 1]))
        tau = yrecv[k, 2] + link * link * inv * tau
    carry = jnp.zeros((nx, nz), jnp.float32)
    zeta, xi = carry, carry
    for k in range(dy - 1, -1, -1):
        xi = jnp.where(k == my, carry, xi)
        carry = invs[k] * (yall[k, 1] + yrecv[k, 1] * carries[k] + yrecv[k, 0] * carry)
        zeta = jnp.where(k == my, carries[k] - taus[k] * carry, zeta)

    for r in range(nx):
        v = (
            xl[r]
            + cbt[:, 4 * nx + r : 4 * nx + r + 1] * zeta[r : r + 1]
            + cbt[:, 5 * nx + r : 5 * nx + r + 1] * xi[r : r + 1]
        )
        v = v / (1.0 + cbt[:, nx + r : nx + r + 1] * mu)
        out[r] = u[r] + lax.dot_general(
            v, basis, (((1,), (1,)), ((), ())),
            precision=lax.Precision.HIGHEST, preferred_element_type=jnp.float32,
        )


def shards(dx, dy, u, p, q, w):
    nx, ny, nz = u.shape
    mode = np.arange(nz)
    basis = np.cos(np.pi * mode[None, :] * (mode[:, None] + 0.5) / nz) * np.sqrt(2.0 / nz)
    basis[:, 0] *= np.sqrt(0.5)
    mu = (2.0 - 2.0 * np.cos(np.pi * mode / nz))[None, :]
    consts = jnp.asarray(np.concatenate([basis, np.repeat(mu, 8, 0)]), jnp.float32)
    chunk = ny // dx
    f32 = lambda *shape: pltpu.VMEM(shape, jnp.float32)
    up = lambda n: -(-n // 128) * 128
    rows, orows = up(6 * nx), up(5 * dx)
    sems = [pltpu.SemaphoreType.DMA((5,))]
    for count in (dx, dy, dy, dx, dx, dy):
        sems += [pltpu.SemaphoreType.DMA((count,))] * 2
    return pl.pallas_call(
        functools.partial(kernel, dx, dy),
        out_shape=jax.ShapeDtypeStruct(u.shape, jnp.float32),
        in_specs=[pl.BlockSpec(memory_space=pltpu.HBM)] * 5,
        out_specs=pl.BlockSpec(memory_space=pltpu.VMEM),
        scratch_shapes=[
            f32(nx, ny, nz), f32(nx, ny), f32(nx, ny), f32(nx, ny), f32(nz + 8, nz),
            f32(nx, ny, nz), f32(nx, ny, nz), f32(3, nx, ny), f32(dy, 3, nx, ny),
            f32(3, nx, nz), f32(dy, 3, nx, nz), f32(8, ny), f32(dx, 8, ny),
            f32(2, ny, nz), f32(dx, 2, chunk, nz), f32(dx, 2, chunk, nz),
            f32(2, ny, nz), f32(2, nx, nz), f32(dy, 2, nx, nz),
            f32(rows, ny), f32(ny, rows), f32(rows, ny), f32(ny, rows),
            f32(orows, ny), f32(ny, orows),
        ] + sems,
        compiler_params=pltpu.CompilerParams(
            collective_id=0, has_side_effects=True, vmem_limit_bytes=48 * 2**20
        ),
    )(u, p, q, w, consts)


def solution(mesh):
    dx, dy = mesh.shape["gx"], mesh.shape["gy"]
    in_specs = (P("gx", "gy", None), P("gx", "gy"), P("gx", "gy"), P("gx", "gy"))
    return jax.shard_map(
        functools.partial(shards, dx, dy), mesh=mesh, in_specs=in_specs,
        out_specs=P("gx", "gy", None), check_vma=False,
    )
```

```python
import functools

import jax
import jax.numpy as jnp
import numpy as np
from jax import lax
from jax.experimental import pallas as pl
from jax.experimental.pallas import tpu as pltpu
from jax.sharding import PartitionSpec as P

R1 = 40000.0
R2 = 40000.0
R3 = 0.25
MESH = pl.DeviceIdType.MESH


def dot(a, b):
    return jnp.dot(a, b, precision=lax.Precision.HIGHEST, preferred_element_type=jnp.float32)


def kernel(
    dx, dy,
    u_h, p_h, q_h, w_h, consts_h, out,
    u, p, q, w, consts,
    uh, xl, gbuf, grecv, ybuf, yrecv, nbuf, nrecv, summ, rin, rout, zx, ysum, yall,
    ca, cat, cb, cbt, co, cot,
    in_sem, n_send, n_recv, g_send, g_recv, c_send, c_recv,
    a_send, a_recv, b_send, b_recv, y_send, y_recv,
):
    nx, ny, nz = u.shape
    chunk = ny // dx
    mx, my = lax.axis_index("gx"), lax.axis_index("gy")
    far_first = sorted(range(1, dx), key=lambda o: abs(2 * o - dx))

    barrier = pltpu.get_barrier_semaphore()
    for off in far_first:
        pl.semaphore_signal(
            barrier, inc=1, device_id={"gx": lax.rem(mx + off, dx)}, device_id_type=MESH
        )
    for off in range(1, dy):
        pl.semaphore_signal(
            barrier, inc=1, device_id={"gy": lax.rem(my + off, dy)}, device_id_type=MESH
        )
    loads = []
    for k, (src, dst) in enumerate(
        ((q_h, q), (p_h, p), (w_h, w), (consts_h, consts), (u_h, u))
    ):
        loads.append(pltpu.make_async_copy(src, dst, in_sem.at[k]))
        loads[k].start()

    def send(src, dst, ssem, rsem, axis, peer):
        copy = pltpu.make_async_remote_copy(
            src_ref=src, dst_ref=dst, send_sem=ssem, recv_sem=rsem,
            device_id={axis: peer}, device_id_type=MESH,
        )
        copy.start()
        return copy

    for k in range(3):
        loads[k].wait()

    g = R2 * q[...]
    lane = lax.broadcasted_iota(jnp.int32, (nx, ny), 1)
    scale = 1.0 / (2.0 + 3.0 * g)
    a, b, c, d = (1.0 + g) * scale, g * scale, scale, g * scale
    stride = 1
    while stride < ny:
        ar, br, cr, dr = (pltpu.roll(m, stride, 1) for m in (a, b, c, d))
        na, nb, nc, nd = a * ar + b * cr, a * br + b * dr, c * ar + d * cr, c * br + d * dr
        scale = 1.0 / (na + nb + nc + nd)
        keep = lane >= stride
        a, b, c, d = (
            jnp.where(keep, n * scale, o)
            for n, o in ((na, a), (nb, b), (nc, c), (nd, d))
        )
        stride *= 2
    sigma = jnp.where(lane == 0, 1.0, pltpu.roll((a + b) / (c + d), 1, 1))
    ipi = 1.0 / (g + sigma)
    rho = g * ipi
    prefix = rho
    stride = 1
    while stride < ny:
        prefix = jnp.where(lane >= stride, prefix * pltpu.roll(prefix, stride, 1), prefix)
        stride *= 2
    total = prefix[:, ny - 1 :]
    before = jnp.where(lane == 0, 1.0, pltpu.roll(prefix, 1, 1))
    inverse = 1.0 / before
    row_i = lax.broadcasted_iota(jnp.int32, (ny, ny), 0)
    col_i = lax.broadcasted_iota(jnp.int32, (ny, ny), 1)
    lower = jnp.where(row_i >= col_i, 1.0, 0.0)
    upper = jnp.where(row_i <= col_i, 1.0, 0.0)
    weight = before * before * ipi
    a2 = inverse * dot(weight, lower)
    b2 = inverse * total
    cb[...] = jnp.zeros_like(cb)
    for k, m in enumerate((g, R3 * w[...], inverse, weight, a2, b2)):
        cb[k * nx : (k + 1) * nx] = m
    cbt[...] = cb[...].T
    ybuf[0] = jnp.broadcast_to(total, (nx, nz))
    ybuf[1] = jnp.broadcast_to(a2[:, 0:1], (nx, nz))
    ybuf[2] = jnp.broadcast_to((rho * sigma)[:, ny - 1 :], (nx, nz))

    gp = R1 * p[...]
    sigma = jnp.ones((1, ny), jnp.float32)
    rhos, ipis, prod = [], [], [sigma]
    for r in range(nx):
        gr = gp[r : r + 1]
        inv = 1.0 / (gr + sigma)
        rhos.append(gr * inv)
        ipis.append(inv)
        leak = rhos[r] * sigma
        sigma = 1.0 + leak
        prod.append(prod[r] * rhos[r])
    resp, tail = [None] * nx, [None] * nx
    resp[nx - 1], tail[nx - 1] = prod[nx - 1] * ipis[nx - 1], rhos[nx - 1]
    for r in range(nx - 2, -1, -1):
        resp[r] = prod[r] * ipis[r] + rhos[r] * resp[r + 1]
        tail[r] = rhos[r] * tail[r + 1]
    ca[...] = jnp.zeros_like(ca)
    for k, m in enumerate((rhos, ipis, resp, tail)):
        ca[k * nx : (k + 1) * nx] = jnp.concatenate(m, 0)
    cat[...] = ca[...].T
    nbuf[...] = jnp.zeros_like(nbuf)
    nbuf[0:1] = tail[0]
    nbuf[1:2] = resp[0]
    nbuf[2:3] = leak

    loads[3].wait()
    loads[4].wait()
    basis = consts[0:nz]
    mu = consts[nz : nz + 1]
    gbuf[0] = u[:, 0, :]
    gbuf[1] = u[:, ny - 1, :]
    gbuf[2] = q[...]
    uh[...] = dot(u[...].reshape(nx * ny, nz), basis).reshape(nx, ny, nz)

    pl.semaphore_wait(barrier, dx + dy - 2)
    g_copies = [
        send(gbuf, grecv.at[my], g_send.at[o], g_recv.at[o], "gy", lax.rem(my + o, dy))
        for o in sorted({1, dy - 1})
    ]
    n_copies = [
        send(nbuf, nrecv.at[mx], n_send.at[o], n_recv.at[o], "gx", lax.rem(mx + o, dx))
        for o in far_first
    ]
    c_copies = [
        send(ybuf, yrecv.at[my], c_send.at[o], c_recv.at[o], "gy", lax.rem(my + o, dy))
        for o in range(1, dy)
    ]
    nrecv[mx] = nbuf[...]
    yrecv[my] = ybuf[...]
    first_u = dot(gbuf[0], basis)
    for copy in g_copies:
        copy.wait()

    prev, following = lax.rem(my + dy - 1, dy), lax.rem(my + 1, dy)
    low_u = dot(grecv[prev, 1], basis)
    high_u = jnp.where(my == dy - 1, 0.0, dot(grecv[following, 0], basis))
    q_before = jnp.where(my == 0, 0.0, R2 * grecv[prev, 2][:, ny - 1 :])
    low_flux = q_before * (first_u - low_u)

    row = lax.broadcasted_iota(jnp.int32, (ny, nz), 0)
    z = None
    for r in range(nx):
        v = uh[r]
        gc = cbt[:, r : r + 1]
        wc = cbt[:, nx + r : nx + r + 1]
        after = jnp.where(row == ny - 1, high_u[r : r + 1], pltpu.roll(v, ny - 1, 0))
        flux = gc * (after - v)
        flux_before = jnp.where(row == 0, low_flux[r : r + 1], pltpu.roll(flux, 1, 0))
        h = (flux - flux_before) + (v - (wc * mu) * v)
        z = h if r == 0 else h + cat[:, r - 1 : r] * z
        xl[r] = z
    summ[0] = cat[:, nx - 1 : nx] * z
    x = z * cat[:, 2 * nx - 1 : 2 * nx]
    xl[nx - 1] = x
    for r in range(nx - 2, -1, -1):
        x = xl[r] * cat[:, nx + r : nx + r + 1] + cat[:, r : r + 1] * x
        xl[r] = x
    summ[1] = x

    def part(index):
        return pl.ds(pl.multiple_of(index * chunk, chunk), chunk)

    copies = []
    for o in far_first:
        peer = lax.rem(mx + o, dx)
        copies.append(
            send(summ.at[:, part(peer), :], rin.at[mx], a_send.at[o], a_recv.at[o], "gx", peer)
        )
    rin[mx] = summ[:, part(mx), :]

    for copy in n_copies:
        copy.wait()
    co[...] = jnp.zeros_like(co)
    tau = jnp.zeros((1, ny), jnp.float32)
    for k in range(dx):
        link, answer, leak = nrecv[k, 0:1], nrecv[k, 1:2], nrecv[k, 2:3]
        inv = 1.0 / (1.0 + answer * tau)
        co[5 * k : 5 * k + 1] = link * inv
        co[5 * k + 1 : 5 * k + 2] = link * inv * tau
        co[5 * k + 2 : 5 * k + 3] = inv
        co[5 * k + 3 : 5 * k + 4] = inv * answer
        co[5 * k + 4 : 5 * k + 5] = tau
        tau = leak + link * link * inv * tau
    cot[...] = co[...].T
    own = cot[part(mx), :]
    col = lambda k, m: own[:, 5 * k + m : 5 * k + m + 1]
    for copy in copies:
        copy.wait()
    carry = jnp.zeros((chunk, nz), jnp.float32)
    carries = []
    for k in range(dx):
        carries.append(carry)
        carry = rin[k, 0] + col(k, 0) * carry - col(k, 1) * rin[k, 1]
    carry = jnp.zeros((chunk, nz), jnp.float32)
    for k in range(dx - 1, -1, -1):
        rout[k, 1] = carry
        carry = col(k, 2) * rin[k, 1] + col(k, 3) * carries[k] + col(k, 0) * carry
        rout[k, 0] = carries[k] - col(k, 4) * carry
    copies = []
    for o in far_first:
        peer = lax.rem(mx + o, dx)
        copies.append(
            send(rout.at[peer], zx.at[:, part(mx), :], b_send.at[o], b_recv.at[o], "gx", peer)
        )
    zx[:, part(mx), :] = rout[mx]
    for copy in copies:
        copy.wait()

    for r in range(nx):
        x = (
            xl[r]
            + cat[:, 2 * nx + r : 2 * nx + r + 1] * zx[0]
            + cat[:, 3 * nx + r : 3 * nx + r + 1] * zx[1]
        )
        f = 2.0 * (x - uh[r])
        inv = cbt[:, 2 * nx + r : 2 * nx + r + 1]
        s = dot(lower, inv * f)
        ysum[0, r : r + 1, :] = s[ny - 1 :]
        y = inv * dot(upper, cbt[:, 3 * nx + r : 3 * nx + r + 1] * s)
        ysum[1, r : r + 1, :] = y[0:1]
        xl[r] = y
    copies = [
        send(ysum, yall.at[my], y_send.at[o], y_recv.at[o], "gy", lax.rem(my + o, dy))
        for o in range(1, dy)
    ]
    yall[my] = ysum[...]
    for copy in copies + c_copies:
        copy.wait()
    carry = jnp.zeros((nx, nz), jnp.float32)
    tau, carries, taus, invs = carry, [], [], []
    for k in range(dy):
        link = yrecv[k, 0]
        inv = 1.0 / (1.0 + yrecv[k, 1] * tau)
        carries.append(carry)
        taus.append(tau)
        invs.append(inv)
        carry = link * (yall[k, 0] + inv * (carry - tau * yall[k, 1]))
        tau = yrecv[k, 2] + link * link * inv * tau
    carry = jnp.zeros((nx, nz), jnp.float32)
    zeta, xi = carry, carry
    for k in range(dy - 1, -1, -1):
        xi = jnp.where(k == my, carry, xi)
        carry = invs[k] * (yall[k, 1] + yrecv[k, 1] * carries[k] + yrecv[k, 0] * carry)
        zeta = jnp.where(k == my, carries[k] - taus[k] * carry, zeta)

    for r in range(nx):
        v = (
            xl[r]
            + cbt[:, 4 * nx + r : 4 * nx + r + 1] * zeta[r : r + 1]
            + cbt[:, 5 * nx + r : 5 * nx + r + 1] * xi[r : r + 1]
        )
        v = v / (1.0 + cbt[:, nx + r : nx + r + 1] * mu)
        out[r] = u[r] + lax.dot_general(
            v, basis, (((1,), (1,)), ((), ())),
            precision=lax.Precision.HIGHEST, preferred_element_type=jnp.float32,
        )


def shards(dx, dy, u, p, q, w):
    nx, ny, nz = u.shape
    mode = np.arange(nz)
    basis = np.cos(np.pi * mode[None, :] * (mode[:, None] + 0.5) / nz) * np.sqrt(2.0 / nz)
    basis[:, 0] *= np.sqrt(0.5)
    mu = (2.0 - 2.0 * np.cos(np.pi * mode / nz))[None, :]
    consts = jnp.asarray(np.concatenate([basis, np.repeat(mu, 8, 0)]), jnp.float32)
    chunk = ny // dx
    f32 = lambda *shape: pltpu.VMEM(shape, jnp.float32)
    up = lambda n: -(-n // 128) * 128
    rows, orows = up(6 * nx), up(5 * dx)
    sems = [pltpu.SemaphoreType.DMA((5,))]
    for count in (dx, dy, dy, dx, dx, dy):
        sems += [pltpu.SemaphoreType.DMA((count,))] * 2
    return pl.pallas_call(
        functools.partial(kernel, dx, dy),
        out_shape=jax.ShapeDtypeStruct(u.shape, jnp.float32),
        in_specs=[pl.BlockSpec(memory_space=pltpu.HBM)] * 5,
        out_specs=pl.BlockSpec(memory_space=pltpu.VMEM),
        scratch_shapes=[
            f32(nx, ny, nz), f32(nx, ny), f32(nx, ny), f32(nx, ny), f32(nz + 8, nz),
            f32(nx, ny, nz), f32(nx, ny, nz), f32(3, nx, ny), f32(dy, 3, nx, ny),
            f32(3, nx, nz), f32(dy, 3, nx, nz), f32(8, ny), f32(dx, 8, ny),
            f32(2, ny, nz), f32(dx, 2, chunk, nz), f32(dx, 2, chunk, nz),
            f32(2, ny, nz), f32(2, nx, nz), f32(dy, 2, nx, nz),
            f32(rows, ny), f32(ny, rows), f32(rows, ny), f32(ny, rows),
            f32(orows, ny), f32(ny, orows),
        ] + sems,
        compiler_params=pltpu.CompilerParams(
            collective_id=0, has_side_effects=True, vmem_limit_bytes=60 * 1024 * 2**10
        ),
    )(u, p, q, w, consts)


def solution(mesh):
    dx, dy = mesh.shape["gx"], mesh.shape["gy"]
    in_specs = (P("gx", "gy", None), P("gx", "gy"), P("gx", "gy"), P("gx", "gy"))
    return jax.shard_map(
        functools.partial(shards, dx, dy), mesh=mesh, in_specs=in_specs,
        out_specs=P("gx", "gy", None), check_vma=False,
    )
```

```python
import functools

import jax
import jax.numpy as jnp
import numpy as np
from jax import lax
from jax.experimental import pallas as pl
from jax.experimental.pallas import tpu as pltpu
from jax.sharding import PartitionSpec as P

R1 = 40000.0
R2 = 40000.0
R3 = 0.25
MESH = pl.DeviceIdType.MESH


def dot(a, b):
    return jnp.dot(a, b, precision=lax.Precision.HIGHEST, preferred_element_type=jnp.float32)


def kernel(
    dx, dy,
    u_h, p_h, q_h, w_h, consts_h, out,
    u, p, q, w, consts,
    uh, xl, gbuf, grecv, ybuf, yrecv, nbuf, nrecv, summ, rin, rout, zx, ysum, yall,
    ca, cat, cb, cbt, co, cot,
    in_sem, n_send, n_recv, g_send, g_recv, c_send, c_recv,
    a_send, a_recv, b_send, b_recv, y_send, y_recv,
):
    nx, ny, nz = u.shape
    chunk = ny // dx
    mx, my = lax.axis_index("gx"), lax.axis_index("gy")
    far_first = sorted(range(1, dx), key=lambda o: abs(2 * o - dx))

    barrier = pltpu.get_barrier_semaphore()
    for off in far_first:
        pl.semaphore_signal(
            barrier, inc=1, device_id={"gx": lax.rem(mx + off, dx)}, device_id_type=MESH
        )
    for off in range(1, dy):
        pl.semaphore_signal(
            barrier, inc=1, device_id={"gy": lax.rem(my + off, dy)}, device_id_type=MESH
        )
    loads = []
    for k, (src, dst) in enumerate(
        ((q_h, q), (p_h, p), (w_h, w), (consts_h, consts), (u_h, u))
    ):
        loads.append(pltpu.make_async_copy(src, dst, in_sem.at[k]))
        loads[k].start()

    def send(src, dst, ssem, rsem, axis, peer):
        copy = pltpu.make_async_remote_copy(
            src_ref=src, dst_ref=dst, send_sem=ssem, recv_sem=rsem,
            device_id={axis: peer}, device_id_type=MESH,
        )
        copy.start()
        return copy

    for k in range(3):
        loads[k].wait()

    g = R2 * q[...]
    lane = lax.broadcasted_iota(jnp.int32, (nx, ny), 1)
    scale = 1.0 / (2.0 + 3.0 * g)
    a, b, c, d = (1.0 + g) * scale, g * scale, scale, g * scale
    stride = 1
    while stride < ny:
        ar, br, cr, dr = (pltpu.roll(m, stride, 1) for m in (a, b, c, d))
        na, nb, nc, nd = a * ar + b * cr, a * br + b * dr, c * ar + d * cr, c * br + d * dr
        scale = 1.0 / (na + nb + nc + nd)
        keep = lane >= stride
        a, b, c, d = (
            jnp.where(keep, n * scale, o)
            for n, o in ((na, a), (nb, b), (nc, c), (nd, d))
        )
        stride *= 2
    sigma = jnp.where(lane == 0, 1.0, pltpu.roll((a + b) / (c + d), 1, 1))
    ipi = 1.0 / (g + sigma)
    rho = g * ipi
    prefix = rho
    stride = 1
    while stride < ny:
        prefix = jnp.where(lane >= stride, prefix * pltpu.roll(prefix, stride, 1), prefix)
        stride *= 2
    total = prefix[:, ny - 1 :]
    before = jnp.where(lane == 0, 1.0, pltpu.roll(prefix, 1, 1))
    inverse = 1.0 / before
    row_i = lax.broadcasted_iota(jnp.int32, (ny, ny), 0)
    col_i = lax.broadcasted_iota(jnp.int32, (ny, ny), 1)
    lower = jnp.where(row_i >= col_i, 1.0, 0.0)
    upper = jnp.where(row_i <= col_i, 1.0, 0.0)
    weight = before * before * ipi
    a2 = inverse * dot(weight, lower)
    b2 = inverse * total
    cb[...] = jnp.zeros_like(cb)
    for k, m in enumerate((g, R3 * w[...], inverse, weight, a2, b2)):
        cb[k * nx : (k + 1) * nx] = m
    cbt[...] = cb[...].T
    ybuf[0] = jnp.broadcast_to(total, (nx, nz))
    ybuf[1] = jnp.broadcast_to(a2[:, 0:1], (nx, nz))
    ybuf[2] = jnp.broadcast_to((rho * sigma)[:, ny - 1 :], (nx, nz))

    gp = R1 * p[...]
    sigma = jnp.ones((1, ny), jnp.float32)
    rhos, ipis, prod = [], [], [sigma]
    for r in range(nx):
        gr = gp[r : r + 1]
        inv = 1.0 / (gr + sigma)
        rhos.append(gr * inv)
        ipis.append(inv)
        leak = rhos[r] * sigma
        sigma = 1.0 + leak
        prod.append(prod[r] * rhos[r])
    resp, tail = [None] * nx, [None] * nx
    resp[nx - 1], tail[nx - 1] = prod[nx - 1] * ipis[nx - 1], rhos[nx - 1]
    for r in range(nx - 2, -1, -1):
        resp[r] = prod[r] * ipis[r] + rhos[r] * resp[r + 1]
        tail[r] = rhos[r] * tail[r + 1]
    ca[...] = jnp.zeros_like(ca)
    for k, m in enumerate((rhos, ipis, resp, tail)):
        ca[k * nx : (k + 1) * nx] = jnp.concatenate(m, 0)
    cat[...] = ca[...].T
    nbuf[...] = jnp.zeros_like(nbuf)
    nbuf[0:1] = tail[0]
    nbuf[1:2] = resp[0]
    nbuf[2:3] = leak

    loads[3].wait()
    loads[4].wait()
    basis = consts[0:nz]
    mu = consts[nz : nz + 1]
    gbuf[0] = u[:, 0, :]
    gbuf[1] = u[:, ny - 1, :]
    gbuf[2] = q[...]
    uh[...] = dot(u[...].reshape(nx * ny, nz), basis).reshape(nx, ny, nz)

    def part(index):
        return pl.ds(pl.multiple_of(index * chunk, chunk), chunk)

    def first_part(at, count, low_flux, high_u):
        rows_at = slice(at, at + count)
        row = lax.broadcasted_iota(jnp.int32, (count, nz), 0)
        col = lambda k: cat[rows_at, k : k + 1]
        z = None
        for r in range(nx):
            v = uh[r, rows_at]
            gc = cbt[rows_at, r : r + 1]
            wc = cbt[rows_at, nx + r : nx + r + 1]
            after = jnp.where(row == count - 1, high_u[r : r + 1], pltpu.roll(v, count - 1, 0))
            flux = gc * (after - v)
            below = jnp.where(row == 0, low_flux[r : r + 1], pltpu.roll(flux, 1, 0))
            h = (flux - below) + (v - (wc * mu) * v)
            z = h if r == 0 else h + col(r - 1) * z
            xl[r, rows_at] = z
        summ[0, rows_at] = col(nx - 1) * z
        x = z * col(2 * nx - 1)
        xl[nx - 1, rows_at] = x
        for r in range(nx - 2, -1, -1):
            x = xl[r, rows_at] * col(nx + r) + col(r) * x
            xl[r, rows_at] = x
        summ[1, rows_at] = x

    empty = jnp.zeros((nx, nz), jnp.float32)
    first_part(0, ny, empty, empty)

    pl.semaphore_wait(barrier, dx + dy - 2)
    g_copies = [
        send(gbuf, grecv.at[my], g_send.at[o], g_recv.at[o], "gy", lax.rem(my + o, dy))
        for o in sorted({1, dy - 1})
    ]

    def ends(peer, sem):
        return pltpu.make_async_remote_copy(
            src_ref=summ.at[:, peer * chunk : (peer + 1) * chunk, :], dst_ref=rin.at[mx],
            send_sem=a_send.at[peer], recv_sem=a_recv.at[sem],
            device_id={"gx": peer}, device_id_type=MESH,
        )

    middle = sorted(range(1, dx - 1), key=lambda d: abs(2 * d + 1 - dx))[::-1]
    for peer in middle:
        @pl.when(mx != peer)
        def _():
            ends(peer, mx).start()
    n_copies = [
        send(nbuf, nrecv.at[mx], n_send.at[o], n_recv.at[o], "gx", lax.rem(mx + o, dx))
        for o in far_first
    ]
    c_copies = [
        send(ybuf, yrecv.at[my], c_send.at[o], c_recv.at[o], "gy", lax.rem(my + o, dy))
        for o in range(1, dy)
    ]
    nrecv[mx] = nbuf[...]
    yrecv[my] = ybuf[...]
    first_u = dot(gbuf[0], basis)
    for copy in g_copies:
        copy.wait()

    prev, following = lax.rem(my + dy - 1, dy), lax.rem(my + 1, dy)
    low_u = dot(grecv[prev, 1], basis)
    high_u = jnp.where(my == dy - 1, 0.0, dot(grecv[following, 0], basis))
    q_before = jnp.where(my == 0, 0.0, R2 * grecv[prev, 2][:, ny - 1 :])
    first_part(0, chunk, q_before * (first_u - low_u), uh[:, chunk, :])
    at = ny - chunk
    gap = uh[:, at, :] - uh[:, at - 1, :]
    first_part(at, chunk, R2 * q[:, at - 1 : at] * gap, high_u)
    for peer in (0, dx - 1):
        @pl.when(mx != peer)
        def _():
            ends(peer, mx).start()
    rin[mx] = summ[:, part(mx), :]

    for copy in n_copies:
        copy.wait()
    co[...] = jnp.zeros_like(co)
    tau = jnp.zeros((1, ny), jnp.float32)
    for k in range(dx):
        link, answer, leak = nrecv[k, 0:1], nrecv[k, 1:2], nrecv[k, 2:3]
        inv = 1.0 / (1.0 + answer * tau)
        co[5 * k : 5 * k + 1] = link * inv
        co[5 * k + 1 : 5 * k + 2] = link * inv * tau
        co[5 * k + 2 : 5 * k + 3] = inv
        co[5 * k + 3 : 5 * k + 4] = inv * answer
        co[5 * k + 4 : 5 * k + 5] = tau
        tau = leak + link * link * inv * tau
    cot[...] = co[...].T
    own = cot[part(mx), :]
    col = lambda k, m: own[:, 5 * k + m : 5 * k + m + 1]
    for peer in range(dx):
        @pl.when(mx != peer)
        def _():
            copy = ends(peer, peer)
            copy.wait_send()
            copy.wait_recv()
    carry = jnp.zeros((chunk, nz), jnp.float32)
    carries = []
    for k in range(dx):
        carries.append(carry)
        carry = rin[k, 0] + col(k, 0) * carry - col(k, 1) * rin[k, 1]
    carry = jnp.zeros((chunk, nz), jnp.float32)
    for k in range(dx - 1, -1, -1):
        rout[k, 1] = carry
        carry = col(k, 2) * rin[k, 1] + col(k, 3) * carries[k] + col(k, 0) * carry
        rout[k, 0] = carries[k] - col(k, 4) * carry
    copies = []
    for o in far_first:
        peer = lax.rem(mx + o, dx)
        copies.append(
            send(rout.at[peer], zx.at[:, part(mx), :], b_send.at[o], b_recv.at[o], "gx", peer)
        )
    zx[:, part(mx), :] = rout[mx]
    for copy in copies:
        copy.wait()

    for r in range(nx):
        x = (
            xl[r]
            + cat[:, 2 * nx + r : 2 * nx + r + 1] * zx[0]
            + cat[:, 3 * nx + r : 3 * nx + r + 1] * zx[1]
        )
        f = 2.0 * (x - uh[r])
        inv = cbt[:, 2 * nx + r : 2 * nx + r + 1]
        s = dot(lower, inv * f)
        ysum[0, r : r + 1, :] = s[ny - 1 :]
        y = inv * dot(upper, cbt[:, 3 * nx + r : 3 * nx + r + 1] * s)
        ysum[1, r : r + 1, :] = y[0:1]
        xl[r] = y
    copies = [
        send(ysum, yall.at[my], y_send.at[o], y_recv.at[o], "gy", lax.rem(my + o, dy))
        for o in range(1, dy)
    ]
    yall[my] = ysum[...]
    for copy in copies + c_copies:
        copy.wait()
    carry = jnp.zeros((nx, nz), jnp.float32)
    tau, carries, taus, invs = carry, [], [], []
    for k in range(dy):
        link = yrecv[k, 0]
        inv = 1.0 / (1.0 + yrecv[k, 1] * tau)
        carries.append(carry)
        taus.append(tau)
        invs.append(inv)
        carry = link * (yall[k, 0] + inv * (carry - tau * yall[k, 1]))
        tau = yrecv[k, 2] + link * link * inv * tau
    carry = jnp.zeros((nx, nz), jnp.float32)
    zeta, xi = carry, carry
    for k in range(dy - 1, -1, -1):
        xi = jnp.where(k == my, carry, xi)
        carry = invs[k] * (yall[k, 1] + yrecv[k, 1] * carries[k] + yrecv[k, 0] * carry)
        zeta = jnp.where(k == my, carries[k] - taus[k] * carry, zeta)

    for r in range(nx):
        v = (
            xl[r]
            + cbt[:, 4 * nx + r : 4 * nx + r + 1] * zeta[r : r + 1]
            + cbt[:, 5 * nx + r : 5 * nx + r + 1] * xi[r : r + 1]
        )
        v = v / (1.0 + cbt[:, nx + r : nx + r + 1] * mu)
        out[r] = u[r] + lax.dot_general(
            v, basis, (((1,), (1,)), ((), ())),
            precision=lax.Precision.HIGHEST, preferred_element_type=jnp.float32,
        )


def shards(dx, dy, u, p, q, w):
    nx, ny, nz = u.shape
    mode = np.arange(nz)
    basis = np.cos(np.pi * mode[None, :] * (mode[:, None] + 0.5) / nz) * np.sqrt(2.0 / nz)
    basis[:, 0] *= np.sqrt(0.5)
    mu = (2.0 - 2.0 * np.cos(np.pi * mode / nz))[None, :]
    consts = jnp.asarray(np.concatenate([basis, np.repeat(mu, 8, 0)]), jnp.float32)
    chunk = ny // dx
    f32 = lambda *shape: pltpu.VMEM(shape, jnp.float32)
    up = lambda n: -(-n // 128) * 128
    rows, orows = up(6 * nx), up(5 * dx)
    sems = [pltpu.SemaphoreType.DMA((5,))]
    for count in (dx, dy, dy, dx, dx, dy):
        sems += [pltpu.SemaphoreType.DMA((count,))] * 2
    return pl.pallas_call(
        functools.partial(kernel, dx, dy),
        out_shape=jax.ShapeDtypeStruct(u.shape, jnp.float32),
        in_specs=[pl.BlockSpec(memory_space=pltpu.HBM)] * 5,
        out_specs=pl.BlockSpec(memory_space=pltpu.VMEM),
        scratch_shapes=[
            f32(nx, ny, nz), f32(nx, ny), f32(nx, ny), f32(nx, ny), f32(nz + 8, nz),
            f32(nx, ny, nz), f32(nx, ny, nz), f32(3, nx, ny), f32(dy, 3, nx, ny),
            f32(3, nx, nz), f32(dy, 3, nx, nz), f32(8, ny), f32(dx, 8, ny),
            f32(2, ny, nz), f32(dx, 2, chunk, nz), f32(dx, 2, chunk, nz),
            f32(2, ny, nz), f32(2, nx, nz), f32(dy, 2, nx, nz),
            f32(rows, ny), f32(ny, rows), f32(rows, ny), f32(ny, rows),
            f32(orows, ny), f32(ny, orows),
        ] + sems,
        compiler_params=pltpu.CompilerParams(
            collective_id=0, has_side_effects=True, vmem_limit_bytes=60 * 1024 * 2**10
        ),
    )(u, p, q, w, consts)


def solution(mesh):
    dx, dy = mesh.shape["gx"], mesh.shape["gy"]
    in_specs = (P("gx", "gy", None), P("gx", "gy"), P("gx", "gy"), P("gx", "gy"))
    return jax.shard_map(
        functools.partial(shards, dx, dy), mesh=mesh, in_specs=in_specs,
        out_specs=P("gx", "gy", None), check_vma=False,
    )
```
